512 devices in a mesh: strata: 128 (over z, x, core), comp: 4 (over y).
Axes of the slice: x: 4, y: 4, z: 16, core: 2. Of those that a mesh axis runs over, the one named last changes fastest.
Arguments:
- start_points: bfloat16 [2, 8, 2097152], P(None, None, 'strata'), may hold values from 0 to 1
- end_points: bfloat16 [2, 8, 2097152], P(None, None, 'strata'), may hold values from 0 to 1
- owner_lists: int32 [2, 16384, 1], P(None, 'strata'), may hold values from 0 to 127; in each aligned block of 128 rows (0 to 127, 128 to 255, ..., all dimensions but the last counted through in order) at most 2 rows name the same one
- local_strata: int32 [2, 16384], P(None, 'strata'), may hold values from 0 to 15
- last_coef: bfloat16 [2048, 64, 512], P('strata', 'comp'), may hold values from -6 to 6
- growth_rates: float32 [64], P('comp'), may hold values from 0.5 to 2
Outputs:
- middle_coef: bfloat16 [2048, 64, 512], P('strata', 'comp')
- first_coef: float32 [2048, 64, 512], P('strata', 'comp')
The draws below stay inside these ranges and needn't reach their ends.
Inputs may be any that keep to these rules, and one draw needn't show every extreme that they name: `owner_lists`: in each step, among the 128 blocks of one index of strata no owner is named more than 2 times, a bound that some block reaches.
All inputs are finite; a program needn't handle non-finite values.
Results may differ from the reference program's by a relative error of at most 0.0075.
The reference program's roundings to bfloat16 on the way count: a program that leaves them out, or rounds other values in their place, can miss the bound.
Values may be sent and summed in bfloat16 or wider, within the bound.
A program may use at most 64 MiB of HBM per device.

```python
import math
import jax
import jax.numpy as jnp
import numpy as np
from jax import lax

DIMS = 8
FEAT = 512
COMPS = 64
BLOCK = 128
STEPS = 2
STRATA_PER_UNIT = 16
PATHS = 1024
STRATA = 2048
OWNERS = 128
BLK_DEV = 128
BLOCKS = 16384
ROWS = 2097152
CAP = 2
N_STRATA = 128


def place_ends(values, own_key, least, top_value):
    shape = values.shape
    spot = [jax.random.randint(jax.random.fold_in(own_key, axis), (), 0, shape[axis]) for axis in range(len(shape))]
    values = values.at[tuple(spot)].set(least)
    longest = shape.index(max(shape))
    spot[longest] = (spot[longest] + 1) % shape[longest]
    return values.at[tuple(spot)].set(top_value)


def block_scale(own_key, extent, pieces, low, high):
    gain = 1.0
    for dim, shards_of in pieces:
        steps = jax.random.uniform(jax.random.fold_in(jax.random.fold_in(own_key, 6), dim), (shards_of,), jnp.float32, low / len(pieces), high / len(pieces))
        gain = gain * jnp.repeat(jnp.exp(steps), extent[dim] // shards_of).reshape((-1,) + (1,) * (len(extent) - 1 - dim))
    return gain


def routed_block(own_key, own, number, rows, amount, top, most, slope):
    sequence = jax.random.permutation(own_key, amount)
    heavy_load, common = portions_of(amount, rows * top, most, slope, True), portions_of(amount, rows * top, most, slope, False)
    places = jnp.arange(amount)

    def named(tallies, offset_by):
        used = int((tallies > 0).sum())
        fixed = max(1, used // 4)
        passed = fixed + (places - fixed + offset_by * (used - fixed)) % max(1, amount - fixed)
        return jnp.zeros((amount,), jnp.int32).at[sequence[jnp.where(places < fixed, places, passed)]].set(jnp.asarray(tallies, jnp.int32))

    tallies = jnp.where(number % 4 == 0, named(heavy_load, number // 4), named(common, number - number // 4 - 1))
    mixed = jax.random.permutation(jax.random.fold_in(own, 3), amount)
    source_of, taker = mixed[0:amount // 2 * 2:2], mixed[1:amount // 2 * 2:2]
    room = jnp.minimum(tallies[source_of] - 1, most - tallies[taker]) // 2
    room = jnp.where((source_of == sequence[0]) | (taker == sequence[0]) | (tallies[taker] == 0), 0, jnp.maximum(room, 0))
    passed = jax.random.randint(jax.random.fold_in(own, 4), (amount // 2,), 0, 1 << 20) % (room + 1)
    tallies = tallies.at[source_of].add(-passed).at[taker].add(passed)
    members = jnp.searchsorted(jnp.cumsum(tallies), jnp.arange(rows * top), side="right").astype(jnp.int32)
    grid = members.reshape(top, rows).T
    grid = grid[jax.random.permutation(jax.random.fold_in(own, 1), rows)]
    offset_by = jax.random.randint(jax.random.fold_in(own, 2), (rows, 1), 0, top)
    return jnp.take_along_axis(grid, (jnp.arange(top)[None, :] + offset_by) % top, axis=1)


def portions_of(count, total, reach, lean, full):
    weights = [(1 << 20) // math.isqrt(rank ** lean) + 1 for rank in range(1, count + 1)]
    largest = reach if full else min(reach, max(-(-total // count), total * weights[0] // sum(weights)))
    least = 1 if total - largest >= count - 1 else 0
    counts, surplus = [largest] + [least] * (count - 1), total - largest - least * (count - 1)
    while surplus > 0:
        movable = [i for i in range(1, count) if counts[i] < largest] or [i for i in range(1, count) if counts[i] < reach]
        whole, remaining = sum([weights[i] for i in movable]), surplus
        for i in movable:
            more = min(reach - counts[i], max(1, remaining * weights[i] // whole), surplus)
            counts[i] = counts[i] + more
            surplus = surplus - more
    return np.array(counts)


def bell_draw(rng, extent, spread, most, shards=(), dtype=jnp.bfloat16):
    level = block_scale(rng, extent, shards, -0.22, 0.18) if shards else 1.0
    drawn = jax.random.normal(rng, extent, jnp.float32) * spread * level
    return jnp.minimum(jnp.maximum(drawn, -most), most).astype(dtype)


def setup_inputs(seed: int = 0) -> dict:
    seeds = jax.random.split(jax.random.key(seed), 7)
    start_points = jnp.clip(1.0 * jax.random.uniform(seeds[0], (STEPS, DIMS, ROWS), jnp.float32) ** block_scale(seeds[0], (STEPS, DIMS, ROWS), ((2, 128),), -0.2, 0.2), 0.0, 1.0).astype(jnp.bfloat16)
    end_points = jnp.clip(1.0 * jax.random.uniform(seeds[1], (STEPS, DIMS, ROWS), jnp.float32) ** block_scale(seeds[1], (STEPS, DIMS, ROWS), ((2, 128),), -0.2, 0.2), 0.0, 1.0).astype(jnp.bfloat16)
    owner_lists_keys = jax.random.split(jax.random.fold_in(seeds[2], 1), STEPS * BLOCKS // BLK_DEV)
    owner_lists_turns = jax.random.permutation(jax.random.fold_in(seeds[2], 3), STEPS * BLOCKS // BLK_DEV)
    owner_lists = jax.vmap(lambda own, number: routed_block(jax.random.fold_in(seeds[2], 2), own, number, BLK_DEV, OWNERS, 1, CAP, 2))(owner_lists_keys, owner_lists_turns).reshape((STEPS, BLOCKS, 1))
    local_strata = place_ends(jax.random.randint(seeds[3], (STEPS, BLOCKS), 0, STRATA_PER_UNIT), jax.random.fold_in(seeds[3], 1), 0, STRATA_PER_UNIT - 1).astype(jnp.int32)
    last_coef = bell_draw(seeds[4], (STRATA, COMPS, FEAT), 1.0, 6.0, ((0, 128), (1, 4)))
    growth_rates = jnp.clip(jnp.exp(math.log(2.0) - 1.3862944 * jax.random.uniform(seeds[5], (COMPS,), jnp.float32) ** block_scale(seeds[5], (COMPS,), ((0, 4),), -0.2, 0.2)), 0.5, 2.0)
    return {"start_points": start_points, "end_points": end_points, "owner_lists": owner_lists, "local_strata": local_strata, "last_coef": last_coef, "growth_rates": growth_rates}


root_three = 3.0 ** 0.5
root_five = 5.0 ** 0.5
root_seven = 7.0 ** 0.5
step_length = 0.25


def legendre(columns):
    centered = 2.0 * columns[0] - 1.0
    features = jnp.stack([jnp.ones_like(centered), root_three * centered, root_five * (1.5 * centered * centered - 0.5), root_seven * (2.5 * centered * centered * centered - 1.5 * centered)], axis=-1)
    for column in columns[1:]:
        factor = root_three * (2.0 * column - 1.0)
        features = jnp.concatenate([features, features * factor[..., None]], axis=-1)
    return (features * (1.0 / features.shape[-1] ** 0.5)).astype(jnp.bfloat16)


def reference(start_points, end_points, owner_lists, local_strata, last_coef, growth_rates):
    coeffs = last_coef
    middle = last_coef
    refitted = None
    for section in range(STEPS):
        end_groups = jnp.transpose(end_points[section].reshape(DIMS, N_STRATA, BLK_DEV, BLOCK), (1, 0, 2, 3))
        start_groups = jnp.transpose(start_points[section].reshape(DIMS, N_STRATA, STRATA_PER_UNIT, PATHS), (1, 0, 2, 3))
        destination = (owner_lists[section, :, 0] * STRATA_PER_UNIT + local_strata[section]).astype(jnp.int32).reshape(N_STRATA, BLK_DEV)

        def device_group(items, coeffs=coeffs):
            end_group, start_group, dest_group = items
            features = legendre([end_group[index].astype(jnp.float32) for index in range(DIMS)])
            picked = coeffs[dest_group].astype(jnp.float32)
            values = jnp.einsum('brk,bck->bcr', features.astype(jnp.float32), picked, precision=lax.Precision.HIGHEST).astype(jnp.bfloat16).astype(jnp.float32)
            mean_square = jnp.sum(values * values, axis=1) / COMPS
            pressure = mean_square / (1.0 + mean_square)
            target = (values + step_length * (growth_rates[None, :, None] * values - values * pressure[:, None, :])).astype(jnp.bfloat16)
            start_features = legendre([start_group[index].astype(jnp.float32) for index in range(DIMS)])
            response_rows = target.reshape(STRATA_PER_UNIT, PATHS // BLOCK, COMPS, BLOCK).astype(jnp.float32)
            initial_rows = start_features.reshape(STRATA_PER_UNIT, PATHS // BLOCK, BLOCK, FEAT).astype(jnp.float32)
            return jnp.einsum('spcr,sprk->sck', response_rows, initial_rows, precision=lax.Precision.HIGHEST) * (FEAT / PATHS)

        refitted = lax.map(device_group, (end_groups, start_groups, destination)).reshape(STRATA, COMPS, FEAT)
        if section == 0:
            middle = refitted.astype(jnp.bfloat16)
            coeffs = middle
    return middle, refitted
```

```python
import math
import jax
import jax.numpy as jnp
from jax import lax
from jax.experimental import pallas as pl
from jax.experimental.pallas import tpu as pltpu
from jax.sharding import PartitionSpec as P

COMPS = 64
BLOCK = 128
STEPS = 2
PATHS = 1024
FEAT = 512

root_three = 3.0**0.5
root_five = 5.0**0.5
root_seven = 7.0**0.5
step_length = 0.25


def sent_together(arrays, axis, split_dim, concat_dim, along):
    columns = [a.reshape(*a.shape[:along], -1) for a in arrays]
    both = jnp.concatenate(columns, axis=along)
    whole, at, finished = (
        lax.all_to_all(both, axis, split_axis=split_dim, concat_axis=concat_dim, tiled=True),
        0,
        [],
    )
    for a, column in zip(arrays, columns):
        section = whole[..., at : at + column.shape[along]]
        finished.append(section.reshape(*section.shape[:along], *a.shape[along:]))
        at += column.shape[along]
    return tuple(finished)


def over_copies(array, axis):
    peers = lax.axis_size(axis)
    spread = lax.all_to_all(
        jnp.broadcast_to(array[None], (peers, *array.shape)), axis, 0, 0, tiled=True
    )
    return spread.sum(axis=0)


def feature_rows(points):
    centered = 2.0 * points - 1.0
    n = points.shape[1]
    row = lax.broadcasted_iota(jnp.int32, (8, n), 0)
    spread = [jnp.broadcast_to(centered[d : d + 1, :], (8, n)) for d in range(8)]
    x = spread[0]
    kind = row % 4
    scale = 1.0 / FEAT**0.5
    first = jnp.where(
        kind == 0,
        scale,
        jnp.where(
            kind == 1,
            (root_three * scale) * x,
            jnp.where(
                kind == 2,
                (root_five * scale) * (1.5 * x * x - 0.5),
                (root_seven * scale) * (2.5 * x * x * x - 1.5 * x),
            ),
        ),
    )
    first = jnp.where(row < 4, first, first * (root_three * spread[1]))
    columns = [first]
    for d in range(2, 8):
        factor = root_three * spread[d]
        columns = columns + [c * factor for c in columns]
    return jnp.concatenate(columns, axis=0).astype(jnp.bfloat16)


def evaluate_kernel(codes, points, coef, out):
    slots = points.shape[0]

    def pair(i, carry):
        a, b = 2 * i, 2 * i + 1
        u = jnp.concatenate([points[a], points[b]], axis=1).astype(jnp.float32)
        features = feature_rows(u)
        rows = jnp.concatenate([coef[codes[a]], coef[codes[b]]], axis=0)
        y = jnp.dot(rows, features, preferred_element_type=jnp.float32)
        c = y.shape[0] // 2
        out[a] = y[:c, :BLOCK].astype(jnp.bfloat16)
        out[b] = y[c:, BLOCK:].astype(jnp.bfloat16)
        return carry

    lax.fori_loop(0, slots // 2, pair, 0)


def evaluate(arrived, codes, coeffs):
    slots = arrived.shape[0]
    vmem = pl.BlockSpec(memory_space=pltpu.VMEM)
    return pl.pallas_call(
        evaluate_kernel,
        out_shape=jax.ShapeDtypeStruct((slots, coeffs.shape[1], BLOCK), jnp.bfloat16),
        in_specs=[pl.BlockSpec(memory_space=pltpu.SMEM), vmem, vmem],
        out_specs=vmem,
        name="evaluate",
    )(codes, arrived, coeffs)


def project_kernel(points, values, squares, rates, out, rounded):
    strata = out.shape[0]
    per = PATHS // BLOCK
    rate = rates[...]

    def one(q, carry):
        first = pl.multiple_of(q * PATHS, PATHS)
        targets = []
        for r in range(per):
            y = values[q * per + r].astype(jnp.float32)
            m = squares[pl.ds(q * per + r, 1), :] * (1.0 / COMPS)
            pressure = m / (1.0 + m)
            targets.append((y + step_length * (rate * y - y * pressure)).astype(jnp.bfloat16))
        acc = None
        for r in range(0, per, 2):
            u = points[:, pl.ds(first + r * BLOCK, 2 * BLOCK)].astype(jnp.float32)
            features = feature_rows(u)
            part = lax.dot_general(
                jnp.concatenate(targets[r : r + 2], axis=1),
                features,
                (((1,), (1,)), ((), ())),
                preferred_element_type=jnp.float32,
            )
            acc = part if acc is None else acc + part
        acc = acc * (FEAT / PATHS)
        out[q] = acc
        rounded[q] = acc.astype(jnp.bfloat16)
        return carry

    lax.fori_loop(0, strata, one, 0)


def project(points, values, squares, rates):
    strata = points.shape[1] // PATHS
    comps = values.shape[1]
    vmem = pl.BlockSpec(memory_space=pltpu.VMEM)
    return pl.pallas_call(
        project_kernel,
        out_shape=(
            jax.ShapeDtypeStruct((strata, comps, FEAT), jnp.float32),
            jax.ShapeDtypeStruct((strata, comps, FEAT), jnp.bfloat16),
        ),
        in_specs=[vmem] * 4,
        out_specs=(vmem, vmem),
        name="project",
    )(points, values, squares, rates)


def per_device(start_points, end_points, owner_lists, local_strata, last_coef, growth_rates):
    n_owner = lax.axis_size("strata")
    dev_blocks = owner_lists.shape[1]
    capacity = max(2, (2 * dev_blocks + n_owner - 1) // n_owner)
    components_local = last_coef.shape[1]
    dim_count = end_points.shape[1]
    slot_total = n_owner * capacity
    block_iota = jnp.arange(dev_blocks, dtype=jnp.int32)
    slot_iota = jnp.arange(slot_total, dtype=jnp.int32)
    rates = jnp.broadcast_to(growth_rates[:, None], (components_local, BLOCK))
    coeffs = last_coef
    middle = last_coef
    refitted = None
    for section in range(STEPS):
        owner_ids = owner_lists[section, :, 0]
        local_ids = local_strata[section]
        same_owner = (owner_ids[:, None] == owner_ids[None, :]) & (
            block_iota[None, :] < block_iota[:, None]
        )
        rank_in_pair = jnp.sum(same_owner.astype(jnp.int32), axis=1)
        slot_index = owner_ids * capacity + rank_in_pair
        placing = slot_index[None, :] == slot_iota[:, None]
        stratum_code = (
            jnp.sum(jnp.where(placing, local_ids[None, :], 0), axis=1)
            .astype(jnp.bfloat16)
            .reshape(n_owner, capacity)
        )
        placing_bf = placing.astype(jnp.bfloat16)
        end_blocks = end_points[section].reshape(dim_count, dev_blocks, BLOCK)
        packed = jnp.einsum(
            "sb,dbr->sdr", placing_bf, end_blocks, preferred_element_type=jnp.float32
        ).astype(jnp.bfloat16)
        packed = packed.reshape(n_owner, capacity, dim_count, BLOCK)
        part_rows = BLOCK // lax.axis_size("comp")
        comp_index = lax.axis_index("comp")
        sliced = lax.dynamic_slice_in_dim(packed, comp_index * part_rows, part_rows, 3)
        arrived, arrived_codes = sent_together((sliced, stratum_code), "strata", 0, 0, 2)
        arrived = lax.all_gather(arrived, "comp", axis=3, tiled=True)
        values = evaluate(
            arrived.reshape(slot_total, dim_count, BLOCK),
            arrived_codes.reshape(slot_total).astype(jnp.int32),
            coeffs,
        )
        returned = lax.all_to_all(
            values.reshape(n_owner, capacity, components_local, BLOCK),
            "strata",
            split_axis=0,
            concat_axis=0,
            tiled=True,
        )
        unpacked = jnp.einsum(
            "sb,scr->bcr",
            placing_bf,
            returned.reshape(slot_total, components_local, BLOCK),
            preferred_element_type=jnp.float32,
        )
        local_square = jnp.sum(unpacked * unpacked, axis=1)
        squares = over_copies(local_square, "comp")
        refitted, rounded = project(
            start_points[section], unpacked.astype(jnp.bfloat16), squares, rates
        )
        if section == 0:
            middle = rounded
            coeffs = middle
    return (middle, refitted)


def solution(mesh):
    in_specs = (
        P(None, None, "strata"),
        P(None, None, "strata"),
        P(None, "strata", None),
        P(None, "strata"),
        P("strata", "comp", None),
        P("comp"),
    )
    out_specs = (P("strata", "comp", None), P("strata", "comp", None))
    return jax.shard_map(
        per_device, mesh=mesh, in_specs=in_specs, out_specs=out_specs, check_vma=False
    )
```

```python
import jax
import jax.numpy as jnp
from jax import lax
from jax.experimental import pallas as pl
from jax.experimental.pallas import tpu as pltpu
from jax.sharding import PartitionSpec as P

COMPS = 64
BLOCK = 128
STEPS = 2
PATHS = 1024
FEAT = 512
DIMS = 8
PLANES = 4
MESH = pl.DeviceIdType.MESH

root_three = 3.0**0.5
root_five = 5.0**0.5
root_seven = 7.0**0.5
step_length = 0.25


def plane_of(s):
    return lax.rem(s, 2) + 2 * lax.rem(s // 8 + lax.rem(s // 2, 4), 2)


def source_at(y, i):
    z = i // 2
    x = lax.rem(y // 2 + z, 2) + 2 * lax.rem(i, 2)
    return z * 8 + x * 2 + lax.rem(y, 2)


def turn(s, j, layers):
    k = j // 2
    m = k // 2 + 1
    dz = jnp.where(k == layers - 1, 0, jnp.where(lax.rem(k, 2) == 0, m, layers - m))
    z = lax.rem(s // 8 + dz, layers)
    return z * 2 + lax.rem(j + lax.rem(s // 2, 4) // 2, 2)


def feature_rows(points):
    centered = 2.0 * points - 1.0
    n = points.shape[1]
    row = lax.broadcasted_iota(jnp.int32, (8, n), 0)
    spread = [jnp.broadcast_to(centered[d : d + 1, :], (8, n)) for d in range(8)]
    x = spread[0]
    kind = row % 4
    scale = 1.0 / FEAT**0.5
    first = jnp.where(
        kind == 0,
        scale,
        jnp.where(
            kind == 1,
            (root_three * scale) * x,
            jnp.where(
                kind == 2,
                (root_five * scale) * (1.5 * x * x - 0.5),
                (root_seven * scale) * (2.5 * x * x * x - 1.5 * x),
            ),
        ),
    )
    first = jnp.where(row < 4, first, first * (root_three * spread[1]))
    columns = [first]
    for d in range(2, 8):
        factor = root_three * spread[d]
        columns = columns + [c * factor for c in columns]
    return jnp.concatenate(columns, axis=0).astype(jnp.bfloat16)


def remote(src, dst, ssem, rsem, device):
    return pltpu.make_async_remote_copy(
        src_ref=src,
        dst_ref=dst,
        send_sem=ssem,
        recv_sem=rsem,
        device_id=device,
        device_id_type=MESH,
    )


def drain(ref, sem):
    pltpu.make_async_copy(ref, ref, sem).wait()


def signal(barrier, device):
    pl.semaphore_signal(barrier, inc=1, device_id=device, device_id_type=MESH)


def send_or_keep(src, dst, ssem, rsem, device, mine):
    @pl.when(jnp.logical_not(mine))
    def _():
        remote(src, dst, ssem, rsem, device).start()

    @pl.when(mine)
    def _():
        pltpu.make_async_copy(src, dst, rsem).start()


def split_blocks(points, blocks):
    @pl.loop(0, blocks.shape[0])
    def _(b):
        blocks[b] = points[:, pl.ds(pl.multiple_of(b * BLOCK, BLOCK), BLOCK)]


def two_blocks(blocks, source, owner):
    return jnp.concatenate([blocks[source[2 * owner + r]] for r in range(2)], axis=0)


def exchange_kernel(
    source, points, table, coef, rates, coords, coef_all, rates_all, packed, blocks, s_p, r_p, s_c, r_c, s_r, r_r
):
    s = lax.axis_index("strata")
    y = lax.axis_index("comp")
    owners = packed.shape[0]
    layers = owners // 8
    members = coords.shape[0]
    own = plane_of(s) == y
    barrier = pltpu.get_barrier_semaphore()

    @pl.loop(0, members)
    def _(i):
        from_s = source_at(y, i)

        @pl.when(from_s != s)
        def _():
            signal(barrier, (from_s, y))

    for d in range(1, PLANES):
        signal(barrier, (s, lax.rem(y + d, PLANES)))

    @pl.when(own)
    def _():
        split_blocks(points, blocks)

        @pl.loop(0, owners)
        def _(o):
            packed[o, 0:16, :] = two_blocks(blocks, source, o)
            packed[o, 16:24, :] = table[...]

        pl.semaphore_wait(barrier, owners - 1 + PLANES - 1)

    @pl.when(jnp.logical_not(own))
    def _():
        pl.semaphore_wait(barrier, PLANES - 1)

    mine = (s // 8) * 2 + lax.rem(s // 2, 4) // 2

    @pl.when(own)
    def _():
        @pl.loop(0, owners)
        def _(j):
            k = j // 8
            m = k // 2 + 1
            dz = jnp.where(k == layers - 1, 0, jnp.where(lax.rem(k, 2) == 0, m, layers - m))
            o = lax.rem(s // 8 + dz, layers) * 8 + lax.rem(s + j, 8)
            send_or_keep(packed.at[o], coords.at[mine], s_p, r_p, (o, y), o == s)

    pltpu.make_async_copy(coef, coef_all.at[y], r_c).start()
    pltpu.make_async_copy(rates, rates_all.at[y], r_r).start()
    for d in range(1, PLANES):
        peer = (s, lax.rem(y + d, PLANES))
        remote(coef, coef_all.at[y], s_c, r_c, peer).start()
        remote(rates, rates_all.at[y], s_r, r_r, peer).start()

    drain(coords, r_p)
    drain(coef_all, r_c)
    drain(rates_all, r_r)
    drain(coef_all.at[pl.ds(0, PLANES - 1)], s_c)
    drain(rates_all.at[pl.ds(0, PLANES - 1)], s_r)

    @pl.when(own)
    def _():
        drain(packed.at[pl.ds(0, owners - 1)], s_p)


def main_kernel(
    codes,
    slots,
    source,
    coords,
    coef_all,
    rates,
    start,
    points,
    middle,
    first,
    feat_e,
    feat_p,
    send0,
    send1,
    recv0,
    recv1,
    coef1,
    packed,
    blocks,
    coords1,
    s_0,
    r_0,
    s_1,
    r_1,
    s_c,
    r_c,
    s_p,
    r_p,
):
    s = lax.axis_index("strata")
    y = lax.axis_index("comp")
    owners = packed.shape[0]
    layers = owners // 8
    members = coords.shape[0]
    strata_here = middle.shape[0]
    local = middle.shape[1]
    per = PATHS // BLOCK
    home = plane_of(s)
    own = home == y
    barrier = pltpu.get_barrier_semaphore()

    @pl.loop(0, owners)
    def _(o):
        @pl.when(jnp.logical_not((o == s) & own))
        def _():
            signal(barrier, (o, home))

    @pl.loop(0, members)
    def _(i):
        from_s = source_at(y, i)

        @pl.when(from_s != s)
        def _():
            signal(barrier, (from_s, y))

    for d in range(1, PLANES):
        signal(barrier, (s, lax.rem(y + d, PLANES)))

    def end_features(arrived):
        @pl.loop(0, members)
        def _(i):
            both = jnp.concatenate([arrived[i, 0:8, :], arrived[i, 8:16, :]], axis=1)
            feat_e[i] = feature_rows(both.astype(jnp.float32))

    def evaluate(i, step, coefs, send):
        for r in range(2):
            code = codes[step, 2 * i + r]
            rows = jnp.concatenate([coefs[c, code] for c in range(PLANES)], axis=0)
            value = jnp.dot(
                rows, feat_e[i, :, r * BLOCK : (r + 1) * BLOCK], preferred_element_type=jnp.float32
            )
            value = value.astype(jnp.bfloat16).astype(jnp.float32)
            square = jnp.sum(value * value, axis=0, keepdims=True) * (1.0 / COMPS)
            pressure = square / (1.0 + square)
            target = value + step_length * (rates[...] * value - value * pressure)
            target = target.astype(jnp.bfloat16)
            for c in range(PLANES):
                send[i, c, r] = target[c * local : (c + 1) * local]

    def give_back(i, send, recv, ssem, rsem):
        to = source_at(y, i)
        for c in range(PLANES):
            part = lax.rem(y + c, PLANES)
            send_or_keep(
                send.at[i, part],
                recv.at[pl.ds(2 * s, 2)],
                ssem,
                rsem,
                (to, part),
                (to == s) & (part == y),
            )

    def start_features(step):
        @pl.loop(0, strata_here * per // 2)
        def _(i):
            at = pl.multiple_of(i * (2 * BLOCK), 2 * BLOCK)
            feat_p[i] = feature_rows(start[step, :, pl.ds(at, 2 * BLOCK)].astype(jnp.float32))

    def refit(q, step, recv):
        acc = None
        for r in range(0, per, 2):
            both = jnp.concatenate(
                [recv[slots[step, q * per + r]], recv[slots[step, q * per + r + 1]]], axis=1
            )
            part = lax.dot_general(
                both,
                feat_p[q * (per // 2) + r // 2],
                (((1,), (1,)), ((), ())),
                preferred_element_type=jnp.float32,
            )
            acc = part if acc is None else acc + part
        return acc * (FEAT / PATHS)

    end_features(coords)

    @pl.loop(0, members)
    def _(i):
        evaluate(i, 0, coef_all, send0)

    @pl.when(own)
    def _():
        split_blocks(points, blocks)

        @pl.loop(0, owners)
        def _(o):
            packed[o] = two_blocks(blocks, source, o)

        pl.semaphore_wait(barrier, 2 * (owners - 1) + PLANES - 1)

    @pl.when(jnp.logical_not(own))
    def _():
        pl.semaphore_wait(barrier, members * PLANES + PLANES - 1)

    @pl.loop(0, members)
    def _(j):
        give_back(turn(s, j, layers), send0, recv0, s_0, r_0)

    mine = (s // 8) * 2 + lax.rem(s // 2, 4) // 2

    @pl.when(own)
    def _():
        @pl.loop(0, owners)
        def _(j):
            o = lax.rem(s + 1 + j, owners)
            send_or_keep(packed.at[o], coords1.at[mine], s_p, r_p, (o, y), o == s)

    start_features(0)
    drain(coords1, r_p)
    end_features(coords1)
    drain(recv0, r_0)

    def share(q):
        for d in range(1, PLANES):
            peer = (s, lax.rem(y + d, PLANES))
            remote(coef1.at[y, q], coef1.at[y, q], s_c, r_c, peer).start()

    @pl.loop(0, strata_here)
    def _(q):
        rounded = refit(q, 0, recv0).astype(jnp.bfloat16)
        middle[q] = rounded
        coef1[y, q] = rounded

        @pl.when(q > 0)
        def _():
            share(q - 1)

    share(strata_here - 1)
    drain(coef1.at[pl.ds(0, PLANES - 1)], r_c)

    @pl.loop(0, members)
    def _(j):
        evaluate(turn(s, j, layers), 1, coef1, send1)

        @pl.when(j > 0)
        def _():
            give_back(turn(s, j - 1, layers), send1, recv1, s_1, r_1)

    give_back(turn(s, members - 1, layers), send1, recv1, s_1, r_1)
    start_features(1)
    drain(recv1, r_1)

    @pl.loop(0, strata_here)
    def _(q):
        first[q] = refit(q, 1, recv1)

    drain(coef1.at[pl.ds(0, PLANES - 1)], s_c)

    @pl.when(own)
    def _():
        drain(packed.at[pl.ds(0, owners - 1)], s_p)
        drain(recv0.at[pl.ds(0, 2 * (owners - 1))], s_0)
        drain(recv1.at[pl.ds(0, 2 * (owners - 1))], s_1)

    @pl.when(jnp.logical_not(own))
    def _():
        drain(recv0, s_0)
        drain(recv1, s_1)


VMEM = pl.BlockSpec(memory_space=pltpu.VMEM)
SMEM = pl.BlockSpec(memory_space=pltpu.SMEM)
DMA = pltpu.SemaphoreType.DMA
LIMIT = 60 * 1024 * 1024


def exchange(source, points, table, coef, rates, owners):
    members = owners // PLANES
    strata_here, local, _ = coef.shape
    return pl.pallas_call(
        exchange_kernel,
        out_shape=(
            jax.ShapeDtypeStruct((members, 24, BLOCK), jnp.bfloat16),
            jax.ShapeDtypeStruct((PLANES, strata_here, local, FEAT), jnp.bfloat16),
            jax.ShapeDtypeStruct((PLANES, local, BLOCK), jnp.float32),
        ),
        in_specs=[SMEM, VMEM, VMEM, VMEM, VMEM],
        out_specs=(VMEM, VMEM, VMEM),
        scratch_shapes=[
            pltpu.VMEM((owners, 24, BLOCK), jnp.bfloat16),
            pltpu.VMEM((points.shape[1] // BLOCK, DIMS, BLOCK), jnp.bfloat16),
        ]
        + [DMA] * 6,
        compiler_params=pltpu.CompilerParams(
            collective_id=0, has_side_effects=True, vmem_limit_bytes=LIMIT
        ),
        name="exchange",
    )(source, points, table, coef, rates)


def main(codes, slots, source, coords, coef_all, rates, start, points, owners):
    members = owners // PLANES
    _, strata_here, local, _ = coef_all.shape
    bf = jnp.bfloat16
    return pl.pallas_call(
        main_kernel,
        out_shape=(
            jax.ShapeDtypeStruct((strata_here, local, FEAT), bf),
            jax.ShapeDtypeStruct((strata_here, local, FEAT), jnp.float32),
        ),
        in_specs=[SMEM] * 3 + [VMEM] * 5,
        out_specs=(VMEM, VMEM),
        scratch_shapes=[
            pltpu.VMEM((members, FEAT, 2 * BLOCK), bf),
            pltpu.VMEM((strata_here * PATHS // (2 * BLOCK), FEAT, 2 * BLOCK), bf),
            pltpu.VMEM((members, PLANES, 2, local, BLOCK), bf),
            pltpu.VMEM((members, PLANES, 2, local, BLOCK), bf),
            pltpu.VMEM((2 * owners, local, BLOCK), bf),
            pltpu.VMEM((2 * owners, local, BLOCK), bf),
            pltpu.VMEM((PLANES, strata_here, local, FEAT), bf),
            pltpu.VMEM((owners, 16, BLOCK), bf),
            pltpu.VMEM((points.shape[1] // BLOCK, DIMS, BLOCK), bf),
            pltpu.VMEM((members, 16, BLOCK), bf),
        ]
        + [DMA] * 8,
        compiler_params=pltpu.CompilerParams(
            collective_id=1, has_side_effects=True, vmem_limit_bytes=LIMIT
        ),
        name="steps",
    )(codes, slots, source, coords, coef_all, rates, start, points)


def per_device(start_points, end_points, owner_lists, local_strata, last_coef, growth_rates):
    owners = lax.axis_size("strata")
    dev_blocks = owner_lists.shape[1]
    local = last_coef.shape[1]
    me = lax.axis_index("strata")
    block_iota = jnp.arange(dev_blocks, dtype=jnp.int32)
    slot_iota = jnp.arange(2 * owners, dtype=jnp.int32)
    rates = jnp.broadcast_to(growth_rates[:, None], (local, BLOCK))

    owner_ids = owner_lists[:, :, 0]
    earlier = (owner_ids[:, :, None] == owner_ids[:, None, :]) & (
        block_iota[None, None, :] < block_iota[None, :, None]
    )
    slots = owner_ids * 2 + jnp.sum(earlier.astype(jnp.int32), axis=2)
    placing = slots[:, None, :] == slot_iota[None, :, None]
    source = jnp.sum(jnp.where(placing, block_iota[None, None, :], 0), axis=2)
    code = jnp.sum(jnp.where(placing, local_strata[:, None, :], 0), axis=2)
    table = code.reshape(STEPS, owners, 2).transpose(0, 2, 1).reshape(2 * STEPS, owners)
    table = jnp.pad(table, ((0, 8 - 2 * STEPS), (0, BLOCK - owners))).astype(jnp.bfloat16)

    coords, coef_all, rates_all = exchange(
        source[0], end_points[0], table, last_coef, rates, owners
    )
    here = jnp.arange(BLOCK, dtype=jnp.int32) == me
    arrived = coords[:, 16 : 16 + 2 * STEPS, :].astype(jnp.float32)
    codes = jnp.sum(jnp.where(here[None, None, :], arrived, 0.0), axis=2).astype(jnp.int32)
    codes = codes.reshape(-1, STEPS, 2).transpose(1, 0, 2).reshape(STEPS, -1)
    return main(
        codes,
        slots,
        source[1],
        coords,
        coef_all,
        rates_all.reshape(PLANES * local, BLOCK),
        start_points,
        end_points[1],
        owners,
    )


def solution(mesh):
    in_specs = (
        P(None, None, "strata"),
        P(None, None, "strata"),
        P(None, "strata", None),
        P(None, "strata"),
        P("strata", "comp", None),
        P("comp"),
    )
    out_specs = (P("strata", "comp", None), P("strata", "comp", None))
    return jax.shard_map(
        per_device, mesh=mesh, in_specs=in_specs, out_specs=out_specs, check_vma=False
    )
```

```python
import functools

import jax
import jax.numpy as jnp
from jax import lax
from jax.experimental import pallas as pl
from jax.experimental.pallas import tpu as pltpu
from jax.sharding import PartitionSpec as P

COMPS = 64
BLOCK = 128
STEPS = 2
PATHS = 1024
FEAT = 512
DIMS = 8
PLANES = 4
ROOM = 4
MESH = pl.DeviceIdType.MESH

root_three = 3.0**0.5
root_five = 5.0**0.5
root_seven = 7.0**0.5
step_length = 0.25


def plane_of(s):
    return lax.rem(s, 2) + 2 * lax.rem(s // 8 + lax.rem(s // 2, 4), 2)


def source_at(y, i):
    z = i // 2
    x = lax.rem(y // 2 + z, 2) + 2 * lax.rem(i, 2)
    return z * 8 + x * 2 + lax.rem(y, 2)


def layer_turn(s, k, layers):
    m = k // 2 + 1
    dz = jnp.where(k == layers - 1, 0, jnp.where(lax.rem(k, 2) == 0, m, layers - m))
    return lax.rem(s // 8 + dz, layers)


def turn(s, j, layers):
    return layer_turn(s, j // 2, layers) * 2 + lax.rem(j + lax.rem(s // 2, 4) // 2, 2)


def feature_rows(points):
    centered = 2.0 * points - 1.0
    n = points.shape[1]
    row = lax.broadcasted_iota(jnp.int32, (8, n), 0)
    spread = [jnp.broadcast_to(centered[d : d + 1, :], (8, n)) for d in range(8)]
    x = spread[0]
    kind = row % 4
    scale = 1.0 / FEAT**0.5
    first = jnp.where(
        kind == 0,
        scale,
        jnp.where(
            kind == 1,
            (root_three * scale) * x,
            jnp.where(
                kind == 2,
                (root_five * scale) * (1.5 * x * x - 0.5),
                (root_seven * scale) * (2.5 * x * x * x - 1.5 * x),
            ),
        ),
    )
    first = jnp.where(row < 4, first, first * (root_three * spread[1]))
    columns = [first]
    for d in range(2, 8):
        factor = root_three * spread[d]
        columns = columns + [c * factor for c in columns]
    return jnp.concatenate(columns, axis=0).astype(jnp.bfloat16)


def remote(src, dst, ssem, rsem, device):
    return pltpu.make_async_remote_copy(
        src_ref=src,
        dst_ref=dst,
        send_sem=ssem,
        recv_sem=rsem,
        device_id=device,
        device_id_type=MESH,
    )


def drain(ref, sem):
    pltpu.make_async_copy(ref, ref, sem).wait()


def signal(barrier, device):
    pl.semaphore_signal(barrier, inc=1, device_id=device, device_id_type=MESH)


def send_or_keep(src, dst, ssem, rsem, device, mine):
    @pl.when(jnp.logical_not(mine))
    def _():
        remote(src, dst, ssem, rsem, device).start()

    @pl.when(mine)
    def _():
        pltpu.make_async_copy(src, dst, rsem).start()


def split_blocks(points, step, blocks):
    @pl.loop(0, blocks.shape[0])
    def _(b):
        blocks[b] = points[step, :, pl.ds(pl.multiple_of(b * BLOCK, BLOCK), BLOCK)]


def two_blocks(blocks, source, owner):
    return jnp.concatenate([blocks[source[2 * owner + r]] for r in range(2)], axis=0)


def exchange_kernel(
    source,
    points,
    table,
    coef,
    rates,
    coords,
    coef_all,
    rates_all,
    tables,
    full,
    packed,
    blocks,
    flag,
    s_p,
    r_p,
    s_c,
    r_c,
    s_r,
    r_r,
    s_t,
    r_t,
    s_f,
    r_f,
):
    s = lax.axis_index("strata")
    y = lax.axis_index("comp")
    owners = packed.shape[0]
    layers = owners // 8
    members = coords.shape[0]
    own = plane_of(s) == y
    barrier = pltpu.get_barrier_semaphore()

    @pl.loop(0, members)
    def _(i):
        from_s = source_at(y, i)

        @pl.when(from_s != s)
        def _():
            signal(barrier, (from_s, y))

    @pl.loop(1, layers)
    def _(k):
        signal(barrier, (lax.rem(s + 8 * k, owners), y))

    for d in range(1, PLANES):
        signal(barrier, (s, lax.rem(y + d, PLANES)))

    @pl.when(own)
    def _():
        split_blocks(points, 0, blocks)

        @pl.loop(0, owners)
        def _(o):
            packed[o, 0:16, :] = two_blocks(blocks, source, o)
            packed[o, 16:24, :] = table[...]

        pl.semaphore_wait(barrier, owners - 1 + layers - 1 + PLANES - 1)

    @pl.when(jnp.logical_not(own))
    def _():
        pl.semaphore_wait(barrier, layers - 1 + PLANES - 1)

    mine = (s // 8) * 2 + lax.rem(s // 2, 4) // 2

    @pl.when(own)
    def _():
        @pl.loop(0, owners)
        def _(j):
            o = layer_turn(s, j // 8, layers) * 8 + lax.rem(s + j, 8)
            send_or_keep(packed.at[o], coords.at[mine], s_p, r_p, (o, y), o == s)

    pltpu.make_async_copy(table, tables.at[s // 8], r_t).start()

    @pl.loop(1, layers)
    def _(k):
        remote(table, tables.at[s // 8], s_t, r_t, (lax.rem(s + 8 * k, owners), y)).start()

    pltpu.make_async_copy(coef, coef_all.at[y], r_c).start()
    pltpu.make_async_copy(rates, rates_all.at[y], r_r).start()
    for d in range(1, PLANES):
        peer = (s, lax.rem(y + d, PLANES))
        remote(coef, coef_all.at[y], s_c, r_c, peer).start()
        remote(rates, rates_all.at[y], s_r, r_r, peer).start()

    drain(coords, r_p)
    most = coords[0, 16:24, :].astype(jnp.float32)
    for i in range(1, members):
        most = jnp.maximum(most, coords[i, 16:24, :].astype(jnp.float32))
    flag[...] = most
    pltpu.make_async_copy(flag, full.at[y], r_f).start()
    for d in range(1, PLANES):
        remote(flag, full.at[y], s_f, r_f, (s, lax.rem(y + d, PLANES))).start()
    drain(tables, r_t)
    drain(tables.at[pl.ds(0, layers - 1)], s_t)
    drain(full, r_f)
    drain(full.at[pl.ds(0, PLANES - 1)], s_f)
    drain(coef_all, r_c)
    drain(rates_all, r_r)
    drain(coef_all.at[pl.ds(0, PLANES - 1)], s_c)
    drain(rates_all.at[pl.ds(0, PLANES - 1)], s_r)

    @pl.when(own)
    def _():
        drain(packed.at[pl.ds(0, owners - 1)], s_p)


def main_kernel(
    room,
    codes,
    slots,
    source,
    lists,
    coords,
    coef_all,
    rates,
    start,
    points,
    middle,
    first,
    feat_e,
    feat_p,
    sends,
    seconds,
    stage0,
    stage1,
    packs,
    recv0,
    recv1,
    coef1,
    packed,
    blocks,
    coords1,
    s_v,
    r_v,
    s_w,
    r_w,
    s_z,
    s_c,
    r_c,
    s_p,
    r_p,
):
    s = lax.axis_index("strata")
    y = lax.axis_index("comp")
    owners = packed.shape[0]
    layers = owners // 8
    members = coords.shape[0]
    strata_here = middle.shape[0]
    local = middle.shape[1]
    per = PATHS // BLOCK
    home = plane_of(s)
    own = home == y
    core = lax.rem(s, 2)
    layer = s // 8
    relay = core == lax.rem(y, 2)
    stages = (stage0, stage1)
    recvs = (recv0, recv1)
    barrier = pltpu.get_barrier_semaphore()

    @pl.loop(0, owners)
    def _(o):
        @pl.when(jnp.logical_not((o == s) & own))
        def _():
            signal(barrier, (o, home))

    @pl.loop(0, 16)
    def _(j):
        peer = layer * 8 + j // 2
        plane = core + 2 * lax.rem(j, 2)

        @pl.when(jnp.logical_not((peer == s) & (plane == y)))
        def _():
            signal(barrier, (peer, plane))

    @pl.loop(1, layers)
    def _(k):
        signal(barrier, (lax.rem(s + 8 * k, owners), y))

    @pl.loop(0, members)
    def _(i):
        from_s = source_at(y, i)

        @pl.when(from_s != s)
        def _():
            signal(barrier, (from_s, y))

    for d in range(1, PLANES):
        signal(barrier, (s, lax.rem(y + d, PLANES)))

    def end_features(arrived):
        @pl.loop(0, members)
        def _(i):
            both = jnp.concatenate([arrived[i, 0:8, :], arrived[i, 8:16, :]], axis=1)
            feat_e[i] = feature_rows(both.astype(jnp.float32))

    def evaluate(i, step, coefs):
        for r in range(2):
            code = codes[step, 2 * i + r]
            rows = jnp.concatenate([coefs[c, code] for c in range(PLANES)], axis=0)
            value = jnp.dot(
                rows, feat_e[i, :, r * BLOCK : (r + 1) * BLOCK], preferred_element_type=jnp.float32
            )
            value = value.astype(jnp.bfloat16).astype(jnp.float32)
            square = jnp.sum(value * value, axis=0, keepdims=True) * (1.0 / COMPS)
            pressure = square / (1.0 + square)
            target = value + step_length * (rates[...] * value - value * pressure)
            target = target.astype(jnp.bfloat16)
            for c in range(PLANES):
                (seconds if r else sends)[step, i, c] = target[c * local : (c + 1) * local]

    def give_first(i, step):
        to = source_at(y, i)
        for c in range(PLANES):
            part = lax.rem(y + c, PLANES)
            send_or_keep(
                sends.at[step, i, part],
                recvs[step].at[s],
                s_v.at[step],
                r_v.at[step],
                (to, part),
                (to == s) & (part == y),
            )

    def give_second(i, step):
        source_of = source_at(y, i)
        to = layer * 8 + lax.rem(source_of, 8)
        for c in range(PLANES):
            part = lax.rem(y + c, PLANES)
            send_or_keep(
                seconds.at[step, i, part],
                stages[step].at[source_of // 8, lax.rem(s, 8)],
                s_w.at[step],
                r_w.at[step],
                (to, part),
                (to == s) & (part == y),
            )

    def pass_on(step):
        drain(stages[step], r_w.at[step])

        @pl.loop(0, layers)
        def _(z):
            for k in range(room):
                packs[step, z, k] = stages[step][z, lists[step, z * 8 + k]]

        @pl.loop(0, layers)
        def _(k):
            z = layer_turn(s, k, layers)
            send_or_keep(
                packs.at[step, z],
                recvs[step].at[pl.ds(owners + layer * room, room)],
                s_z.at[step],
                r_v.at[step],
                (z * 8 + lax.rem(s, 8), y),
                z == layer,
            )

    def start_features(step):
        @pl.loop(0, strata_here * per // 2)
        def _(i):
            at = pl.multiple_of(i * (2 * BLOCK), 2 * BLOCK)
            feat_p[i] = feature_rows(start[step, :, pl.ds(at, 2 * BLOCK)].astype(jnp.float32))

    def refit(q, step):
        acc = None
        for r in range(0, per, 2):
            both = jnp.concatenate(
                [recvs[step][slots[step, q * per + r + h]] for h in range(2)], axis=1
            )
            part = lax.dot_general(
                both,
                feat_p[q * (per // 2) + r // 2],
                (((1,), (1,)), ((), ())),
                preferred_element_type=jnp.float32,
            )
            acc = part if acc is None else acc + part
        return acc * (FEAT / PATHS)

    end_features(coords)

    @pl.loop(0, members)
    def _(i):
        evaluate(i, 0, coef_all)

    @pl.when(own)
    def _():
        split_blocks(points, 1, blocks)

        @pl.loop(0, owners)
        def _(o):
            packed[o] = two_blocks(blocks, source, o)

        pl.semaphore_wait(barrier, 2 * (owners - 1) + 15 + layers - 1 + PLANES - 1)

    @pl.when(relay & jnp.logical_not(own))
    def _():
        pl.semaphore_wait(barrier, owners + 15 + layers - 1 + PLANES - 1)

    @pl.when(jnp.logical_not(relay))
    def _():
        pl.semaphore_wait(barrier, owners + 16 + layers - 1 + PLANES - 1)

    @pl.loop(0, members)
    def _(j):
        give_second(turn(s, j, layers), 0)

    @pl.loop(0, members)
    def _(j):
        give_first(turn(s, j, layers), 0)

    mine = (s // 8) * 2 + lax.rem(s // 2, 4) // 2

    @pl.when(own)
    def _():
        @pl.loop(0, owners)
        def _(j):
            o = lax.rem(s + 1 + j, owners)
            send_or_keep(packed.at[o], coords1.at[mine], s_p, r_p, (o, y), o == s)

    pass_on(0)
    start_features(0)
    drain(coords1, r_p)
    end_features(coords1)
    drain(recv0, r_v.at[0])

    def share(q):
        for d in range(1, PLANES):
            peer = (s, lax.rem(y + d, PLANES))
            remote(coef1.at[y, q], coef1.at[y, q], s_c, r_c, peer).start()

    @pl.loop(0, strata_here)
    def _(q):
        rounded = refit(q, 0).astype(jnp.bfloat16)
        middle[q] = rounded
        coef1[y, q] = rounded

        @pl.when(q > 0)
        def _():
            share(q - 1)

    share(strata_here - 1)
    drain(coef1.at[pl.ds(0, PLANES - 1)], r_c)

    @pl.loop(0, members)
    def _(j):
        evaluate(turn(s, j, layers), 1, coef1)

        @pl.when(j > 0)
        def _():
            give_second(turn(s, j - 1, layers), 1)
            give_first(turn(s, j - 1, layers), 1)

    give_second(turn(s, members - 1, layers), 1)
    give_first(turn(s, members - 1, layers), 1)
    pass_on(1)
    start_features(1)
    drain(recv1, r_v.at[1])

    @pl.loop(0, strata_here)
    def _(q):
        first[q] = refit(q, 1)

    drain(coef1.at[pl.ds(0, PLANES - 1)], s_c)

    for step in range(STEPS):
        drain(packs.at[step, pl.ds(0, layers - 1)], s_z.at[step])

        @pl.when(own)
        def _():
            drain(recvs[step].at[pl.ds(0, owners - 1)], s_v.at[step])

        @pl.when(jnp.logical_not(own))
        def _():
            drain(recvs[step].at[pl.ds(0, owners)], s_v.at[step])

        @pl.when(relay)
        def _():
            drain(recvs[step].at[pl.ds(0, owners - layers // 2)], s_w.at[step])

        @pl.when(jnp.logical_not(relay))
        def _():
            drain(recvs[step].at[pl.ds(0, owners)], s_w.at[step])

    @pl.when(own)
    def _():
        drain(packed.at[pl.ds(0, owners - 1)], s_p)


VMEM = pl.BlockSpec(memory_space=pltpu.VMEM)
SMEM = pl.BlockSpec(memory_space=pltpu.SMEM)
DMA = pltpu.SemaphoreType.DMA
LIMIT = 60 * 1024 * 1024


def exchange(source, points, table, coef, rates, owners):
    members = owners // PLANES
    strata_here, local, _ = coef.shape
    return pl.pallas_call(
        exchange_kernel,
        out_shape=(
            jax.ShapeDtypeStruct((members, 24, BLOCK), jnp.bfloat16),
            jax.ShapeDtypeStruct((PLANES, strata_here, local, FEAT), jnp.bfloat16),
            jax.ShapeDtypeStruct((PLANES, local, BLOCK), jnp.float32),
            jax.ShapeDtypeStruct((owners // 8, 8, BLOCK), jnp.bfloat16),
            jax.ShapeDtypeStruct((PLANES, 8, BLOCK), jnp.float32),
        ),
        in_specs=[SMEM, VMEM, VMEM, VMEM, VMEM],
        out_specs=(VMEM,) * 5,
        scratch_shapes=[
            pltpu.VMEM((owners, 24, BLOCK), jnp.bfloat16),
            pltpu.VMEM((points.shape[2] // BLOCK, DIMS, BLOCK), jnp.bfloat16),
            pltpu.VMEM((8, BLOCK), jnp.float32),
        ]
        + [DMA] * 10,
        compiler_params=pltpu.CompilerParams(
            collective_id=0, has_side_effects=True, vmem_limit_bytes=LIMIT
        ),
        name="exchange",
    )(source, points, table, coef, rates)


def main(room, codes, slots, source, lists, coords, coef_all, rates, start, points, owners):
    layers = owners // 8
    members = owners // PLANES
    _, strata_here, local, _ = coef_all.shape
    bf = jnp.bfloat16
    return pl.pallas_call(
        functools.partial(main_kernel, room),
        out_shape=(
            jax.ShapeDtypeStruct((strata_here, local, FEAT), bf),
            jax.ShapeDtypeStruct((strata_here, local, FEAT), jnp.float32),
        ),
        in_specs=[SMEM] * 4 + [VMEM] * 5,
        out_specs=(VMEM, VMEM),
        scratch_shapes=[
            pltpu.VMEM((members, FEAT, 2 * BLOCK), bf),
            pltpu.VMEM((strata_here * PATHS // (2 * BLOCK), FEAT, 2 * BLOCK), bf),
            pltpu.VMEM((STEPS, members, PLANES, local, BLOCK), bf),
            pltpu.VMEM((STEPS, members, PLANES, local, BLOCK), bf),
            pltpu.VMEM((layers, 8, local, BLOCK), bf),
            pltpu.VMEM((layers, 8, local, BLOCK), bf),
            pltpu.VMEM((STEPS, layers, room, local, BLOCK), bf),
            pltpu.VMEM((owners + layers * room, local, BLOCK), bf),
            pltpu.VMEM((owners + layers * room, local, BLOCK), bf),
            pltpu.VMEM((PLANES, strata_here, local, FEAT), bf),
            pltpu.VMEM((owners, 16, BLOCK), bf),
            pltpu.VMEM((points.shape[2] // BLOCK, DIMS, BLOCK), bf),
            pltpu.VMEM((members, 16, BLOCK), bf),
        ]
        + [DMA((STEPS,))] * 5
        + [DMA] * 4,
        compiler_params=pltpu.CompilerParams(
            collective_id=room, has_side_effects=True, vmem_limit_bytes=LIMIT
        ),
        name="steps",
    )(codes, slots, source, lists, coords, coef_all, rates, start, points)


def per_device(start_points, end_points, owner_lists, local_strata, last_coef, growth_rates):
    owners = lax.axis_size("strata")
    dev_blocks = owner_lists.shape[1]
    local = last_coef.shape[1]
    me = lax.axis_index("strata")
    block_iota = jnp.arange(dev_blocks, dtype=jnp.int32)
    slot_iota = jnp.arange(2 * owners, dtype=jnp.int32)
    rates = jnp.broadcast_to(growth_rates[:, None], (local, BLOCK))

    layers = owners // 8
    owner_ids = owner_lists[:, :, 0]
    earlier = (owner_ids[:, :, None] == owner_ids[:, None, :]) & (
        block_iota[None, None, :] < block_iota[None, :, None]
    )
    second = jnp.sum(earlier.astype(jnp.int32), axis=2)
    slots = owner_ids * 2 + second
    placing = slots[:, None, :] == slot_iota[None, :, None]
    source = jnp.sum(jnp.where(placing, block_iota[None, None, :], 0), axis=2)
    code = jnp.sum(jnp.where(placing, local_strata[:, None, :], 0), axis=2)
    ahead = (
        (second[:, None, :] == 1)
        & (owner_ids[:, :, None] // 8 == owner_ids[:, None, :] // 8)
        & (owner_ids[:, None, :] < owner_ids[:, :, None])
    )
    place = jnp.sum(ahead.astype(jnp.int32), axis=2)
    entry = jnp.where(second == 1, owner_ids // 8 * 8 + place, -1)
    listing = entry[:, None, :] == jnp.arange(owners, dtype=jnp.int32)[None, :, None]
    lists = jnp.sum(jnp.where(listing, owner_ids[:, None, :] % 8, 0), axis=2)
    over = jnp.max(jnp.where(second == 1, place, 0)) >= ROOM
    table = code.reshape(STEPS, owners, 2).transpose(0, 2, 1).reshape(2 * STEPS, owners)
    table = jnp.concatenate(
        [table, lists, jnp.broadcast_to(over.astype(jnp.int32), (2, owners))], axis=0
    )
    table = jnp.pad(table, ((0, 0), (0, BLOCK - owners))).astype(jnp.bfloat16)

    coords, coef_all, rates_all, tables, full = exchange(
        source[0], end_points, table, last_coef, rates, owners
    )
    here = jnp.arange(BLOCK, dtype=jnp.int32) == me
    arrived = coords[:, 16 : 16 + 2 * STEPS, :].astype(jnp.float32)
    codes = jnp.sum(jnp.where(here[None, None, :], arrived, 0.0), axis=2).astype(jnp.int32)
    codes = codes.reshape(-1, STEPS, 2).transpose(1, 0, 2).reshape(STEPS, -1)
    wanted = tables[:, 2 * STEPS : 3 * STEPS, :owners].astype(jnp.float32)
    wanted = wanted.reshape(layers, STEPS, layers, 8)
    at_layer = jnp.arange(layers, dtype=jnp.int32) == me // 8
    wanted = jnp.sum(jnp.where(at_layer[None, None, :, None], wanted, 0.0), axis=2)
    wanted = wanted.astype(jnp.int32).transpose(1, 0, 2).reshape(STEPS, layers * 8)
    crowded = jnp.max(full[:, 3 * STEPS, :]) > 0.5

    def run(room):
        index = jnp.where(second == 1, owners + owner_ids // 8 * room + place, owner_ids)
        return main(
            room,
            codes,
            index,
            source[1],
            wanted,
            coords,
            coef_all,
            rates_all.reshape(PLANES * local, BLOCK),
            start_points,
            end_points,
            owners,
        )

    return lax.cond(crowded, lambda: run(8), lambda: run(ROOM))


def solution(mesh):
    in_specs = (
        P(None, None, "strata"),
        P(None, None, "strata"),
        P(None, "strata", None),
        P(None, "strata"),
        P("strata", "comp", None),
        P("comp"),
    )
    out_specs = (P("strata", "comp", None), P("strata", "comp", None))
    return jax.shard_map(
        per_device, mesh=mesh, in_specs=in_specs, out_specs=out_specs, check_vma=False
    )
```

```python
import functools

import jax
import jax.numpy as jnp
from jax import lax
from jax.experimental import pallas as pl
from jax.experimental.pallas import tpu as pltpu
from jax.sharding import PartitionSpec as P

COMPS = 64
BLOCK = 128
STEPS = 2
PATHS = 1024
FEAT = 512
DIMS = 8
PLANES = 4
ROOM = 4
MESH = pl.DeviceIdType.MESH

root_three = 3.0**0.5
root_five = 5.0**0.5
root_seven = 7.0**0.5
step_length = 0.25


def plane_of(s):
    return lax.rem(s, 2) + 2 * lax.rem(s // 8 + lax.rem(s // 2, 4), 2)


def source_at(y, i):
    z = i // 2
    x = lax.rem(y // 2 + z, 2) + 2 * lax.rem(i, 2)
    return z * 8 + x * 2 + lax.rem(y, 2)


def layer_turn(s, k, layers):
    m = k // 2 + 1
    dz = jnp.where(k == layers - 1, 0, jnp.where(lax.rem(k, 2) == 0, m, layers - m))
    return lax.rem(s // 8 + dz, layers)


def turn(s, j, layers):
    return layer_turn(s, j // 2, layers) * 2 + lax.rem(j + lax.rem(s // 2, 4) // 2, 2)


def feature_rows(points):
    centered = 2.0 * points - 1.0
    n = points.shape[1]
    row = lax.broadcasted_iota(jnp.int32, (8, n), 0)
    spread = [jnp.broadcast_to(centered[d : d + 1, :], (8, n)) for d in range(8)]
    x = spread[0]
    kind = row % 4
    scale = 1.0 / FEAT**0.5
    first = jnp.where(
        kind == 0,
        scale,
        jnp.where(
            kind == 1,
            (root_three * scale) * x,
            jnp.where(
                kind == 2,
                (root_five * scale) * (1.5 * x * x - 0.5),
                (root_seven * scale) * (2.5 * x * x * x - 1.5 * x),
            ),
        ),
    )
    first = jnp.where(row < 4, first, first * (root_three * spread[1]))
    columns = [first]
    for d in range(2, 8):
        factor = root_three * spread[d]
        columns = columns + [c * factor for c in columns]
    return jnp.concatenate(columns, axis=0).astype(jnp.bfloat16)


def remote(src, dst, ssem, rsem, device):
    return pltpu.make_async_remote_copy(
        src_ref=src,
        dst_ref=dst,
        send_sem=ssem,
        recv_sem=rsem,
        device_id=device,
        device_id_type=MESH,
    )


def drain(ref, sem):
    pltpu.make_async_copy(ref, ref, sem).wait()


def signal(barrier, device):
    pl.semaphore_signal(barrier, inc=1, device_id=device, device_id_type=MESH)


def send_or_keep(src, dst, ssem, rsem, device, mine):
    @pl.when(jnp.logical_not(mine))
    def _():
        remote(src, dst, ssem, rsem, device).start()

    @pl.when(mine)
    def _():
        pltpu.make_async_copy(src, dst, rsem).start()


def pass_around(table, s, y, half, ssem, rsems):
    above, below = lax.rem(y + 1, PLANES), lax.rem(y + PLANES - 1, PLANES)
    up = table.at[below, pl.ds(0, half)]
    drain(up, rsems.at[0])
    remote(up, up, ssem, rsems.at[4], (s, above)).start()
    down = table.at[above, pl.ds(half, half)]
    drain(down, rsems.at[3])
    remote(down, down, ssem, rsems.at[5], (s, below)).start()


def gathered(table, y, half, rsems):
    above, below = lax.rem(y + 1, PLANES), lax.rem(y + PLANES - 1, PLANES)
    across = lax.rem(y + 2, PLANES)
    drain(table.at[below, pl.ds(half, half)], rsems.at[1])
    drain(table.at[above, pl.ds(0, half)], rsems.at[2])
    drain(table.at[across, pl.ds(0, half)], rsems.at[4])
    drain(table.at[across, pl.ds(half, half)], rsems.at[5])


def split_blocks(points, step, blocks):
    @pl.loop(0, blocks.shape[0])
    def _(b):
        blocks[b] = points[step, :, pl.ds(pl.multiple_of(b * BLOCK, BLOCK), BLOCK)]


def two_blocks(blocks, source, owner):
    return jnp.concatenate([blocks[source[2 * owner + r]] for r in range(2)], axis=0)


def exchange_kernel(
    source,
    points,
    table,
    coef,
    rates,
    coords,
    coef_all,
    rates_all,
    tables,
    full,
    packed,
    blocks,
    flag,
    s_p,
    r_p,
    s_c,
    r_c,
    s_r,
    r_r,
    s_t,
    r_t,
    s_f,
    r_f,
    r_g,
):
    s = lax.axis_index("strata")
    y = lax.axis_index("comp")
    owners = packed.shape[0]
    layers = owners // 8
    members = coords.shape[0]
    own = plane_of(s) == y
    barrier = pltpu.get_barrier_semaphore()

    @pl.loop(0, members)
    def _(i):
        from_s = source_at(y, i)

        @pl.when(from_s != s)
        def _():
            signal(barrier, (from_s, y))

    @pl.loop(1, layers)
    def _(k):
        signal(barrier, (lax.rem(s + 8 * k, owners), y))

    for d in range(1, PLANES):
        signal(barrier, (s, lax.rem(y + d, PLANES)))

    @pl.when(own)
    def _():
        split_blocks(points, 0, blocks)

        @pl.loop(0, owners)
        def _(o):
            packed[o, 0:16, :] = two_blocks(blocks, source, o)
            packed[o, 16:24, :] = table[...]

        pl.semaphore_wait(barrier, owners - 1 + layers - 1 + PLANES - 1)

    @pl.when(jnp.logical_not(own))
    def _():
        pl.semaphore_wait(barrier, layers - 1 + PLANES - 1)

    mine = (s // 8) * 2 + lax.rem(s // 2, 4) // 2

    @pl.when(own)
    def _():
        @pl.loop(0, owners)
        def _(j):
            o = layer_turn(s, j // 8, layers) * 8 + lax.rem(s + j, 8)
            send_or_keep(packed.at[o], coords.at[mine], s_p, r_p, (o, y), o == s)

    pltpu.make_async_copy(table, tables.at[s // 8], r_t).start()

    @pl.loop(1, layers)
    def _(k):
        remote(table, tables.at[s // 8], s_t, r_t, (lax.rem(s + 8 * k, owners), y)).start()

    own_copy = pltpu.make_async_copy(coef, coef_all.at[y], r_c)
    own_copy.start()
    pltpu.make_async_copy(rates, rates_all.at[y], r_r).start()
    for d in range(1, PLANES):
        peer = (s, lax.rem(y + d, PLANES))
        remote(rates, rates_all.at[y], s_r, r_r, peer).start()
    half = coef.shape[0] // 2
    above, below = lax.rem(y + 1, PLANES), lax.rem(y + PLANES - 1, PLANES)
    low, high = pl.ds(0, half), pl.ds(half, half)
    for part, at in ((low, 0), (high, 1)):
        remote(coef.at[part], coef_all.at[y, part], s_c, r_g.at[at], (s, above)).start()
    for part, at in ((high, 3), (low, 2)):
        remote(coef.at[part], coef_all.at[y, part], s_c, r_g.at[at], (s, below)).start()
    pass_around(coef_all, s, y, half, s_c, r_g)

    drain(coords, r_p)
    most = coords[0, 16:24, :].astype(jnp.float32)
    for i in range(1, members):
        most = jnp.maximum(most, coords[i, 16:24, :].astype(jnp.float32))
    flag[...] = most
    pltpu.make_async_copy(flag, full.at[y], r_f).start()
    for d in range(1, PLANES):
        remote(flag, full.at[y], s_f, r_f, (s, lax.rem(y + d, PLANES))).start()
    drain(tables, r_t)
    drain(tables.at[pl.ds(0, layers - 1)], s_t)
    drain(full, r_f)
    drain(full.at[pl.ds(0, PLANES - 1)], s_f)
    own_copy.wait()
    gathered(coef_all, y, half, r_g)
    drain(rates_all, r_r)
    drain(coef_all.at[pl.ds(0, PLANES - 1)], s_c)
    drain(rates_all.at[pl.ds(0, PLANES - 1)], s_r)

    @pl.when(own)
    def _():
        drain(packed.at[pl.ds(0, owners - 1)], s_p)


def main_kernel(
    room,
    codes,
    slots,
    source,
    lists,
    coords,
    coef_all,
    rates,
    start,
    points,
    middle,
    first,
    feat_e,
    feat_p,
    sends,
    seconds,
    stage0,
    stage1,
    packs,
    recv0,
    recv1,
    coef1,
    packed,
    blocks,
    coords1,
    s_v,
    r_v,
    s_w,
    r_w,
    s_z,
    s_c,
    r_c,
    s_p,
    r_p,
):
    s = lax.axis_index("strata")
    y = lax.axis_index("comp")
    owners = packed.shape[0]
    layers = owners // 8
    members = coords.shape[0]
    strata_here = middle.shape[0]
    local = middle.shape[1]
    per = PATHS // BLOCK
    home = plane_of(s)
    own = home == y
    core = lax.rem(s, 2)
    layer = s // 8
    relay = core == lax.rem(y, 2)
    stages = (stage0, stage1)
    recvs = (recv0, recv1)
    barrier = pltpu.get_barrier_semaphore()

    @pl.loop(0, owners)
    def _(o):
        @pl.when(jnp.logical_not((o == s) & own))
        def _():
            signal(barrier, (o, home))

    @pl.loop(0, 16)
    def _(j):
        peer = layer * 8 + j // 2
        plane = core + 2 * lax.rem(j, 2)

        @pl.when(jnp.logical_not((peer == s) & (plane == y)))
        def _():
            signal(barrier, (peer, plane))

    @pl.loop(1, layers)
    def _(k):
        signal(barrier, (lax.rem(s + 8 * k, owners), y))

    @pl.loop(0, members)
    def _(i):
        from_s = source_at(y, i)

        @pl.when(from_s != s)
        def _():
            signal(barrier, (from_s, y))

    for d in range(1, PLANES):
        signal(barrier, (s, lax.rem(y + d, PLANES)))

    def end_features(arrived):
        @pl.loop(0, members)
        def _(i):
            both = jnp.concatenate([arrived[i, 0:8, :], arrived[i, 8:16, :]], axis=1)
            feat_e[i] = feature_rows(both.astype(jnp.float32))

    def evaluate(i, step, coefs):
        for r in range(2):
            code = codes[step, 2 * i + r]
            rows = jnp.concatenate([coefs[c, code] for c in range(PLANES)], axis=0)
            value = jnp.dot(
                rows, feat_e[i, :, r * BLOCK : (r + 1) * BLOCK], preferred_element_type=jnp.float32
            )
            value = value.astype(jnp.bfloat16).astype(jnp.float32)
            square = jnp.sum(value * value, axis=0, keepdims=True) * (1.0 / COMPS)
            pressure = square / (1.0 + square)
            target = value + step_length * (rates[...] * value - value * pressure)
            target = target.astype(jnp.bfloat16)
            for c in range(PLANES):
                (seconds if r else sends)[step, i, c] = target[c * local : (c + 1) * local]

    def give_first(i, step):
        to = source_at(y, i)
        for c in range(PLANES):
            part = lax.rem(y + c, PLANES)
            send_or_keep(
                sends.at[step, i, part],
                recvs[step].at[s],
                s_v.at[step],
                r_v.at[step],
                (to, part),
                (to == s) & (part == y),
            )

    def give_second(i, step):
        source_of = source_at(y, i)
        to = layer * 8 + lax.rem(source_of, 8)
        for c in range(PLANES):
            part = lax.rem(y + c, PLANES)
            send_or_keep(
                seconds.at[step, i, part],
                stages[step].at[source_of // 8, lax.rem(s, 8)],
                s_w.at[step],
                r_w.at[step],
                (to, part),
                (to == s) & (part == y),
            )

    def pass_on(step):
        drain(stages[step], r_w.at[step])

        @pl.loop(0, layers)
        def _(z):
            for k in range(room):
                packs[step, z, k] = stages[step][z, lists[step, z * 8 + k]]

        @pl.loop(0, layers)
        def _(k):
            z = layer_turn(s, k, layers)
            send_or_keep(
                packs.at[step, z],
                recvs[step].at[pl.ds(owners + layer * room, room)],
                s_z.at[step],
                r_v.at[step],
                (z * 8 + lax.rem(s, 8), y),
                z == layer,
            )

    def start_features(step):
        @pl.loop(0, strata_here * per // 2)
        def _(i):
            at = pl.multiple_of(i * (2 * BLOCK), 2 * BLOCK)
            feat_p[i] = feature_rows(start[step, :, pl.ds(at, 2 * BLOCK)].astype(jnp.float32))

    def refit(q, step):
        acc = None
        for r in range(0, per, 2):
            both = jnp.concatenate(
                [recvs[step][slots[step, q * per + r + h]] for h in range(2)], axis=1
            )
            part = lax.dot_general(
                both,
                feat_p[q * (per // 2) + r // 2],
                (((1,), (1,)), ((), ())),
                preferred_element_type=jnp.float32,
            )
            acc = part if acc is None else acc + part
        return acc * (FEAT / PATHS)

    end_features(coords)

    @pl.loop(0, members)
    def _(i):
        evaluate(i, 0, coef_all)

    @pl.when(own)
    def _():
        split_blocks(points, 1, blocks)

        @pl.loop(0, owners)
        def _(o):
            packed[o] = two_blocks(blocks, source, o)

        pl.semaphore_wait(barrier, 2 * (owners - 1) + 15 + layers - 1 + PLANES - 1)

    @pl.when(relay & jnp.logical_not(own))
    def _():
        pl.semaphore_wait(barrier, owners + 15 + layers - 1 + PLANES - 1)

    @pl.when(jnp.logical_not(relay))
    def _():
        pl.semaphore_wait(barrier, owners + 16 + layers - 1 + PLANES - 1)

    @pl.loop(0, members)
    def _(j):
        give_second(turn(s, j, layers), 0)

    @pl.loop(0, members)
    def _(j):
        give_first(turn(s, j, layers), 0)

    mine = (s // 8) * 2 + lax.rem(s // 2, 4) // 2

    @pl.when(own)
    def _():
        @pl.loop(0, owners)
        def _(j):
            o = lax.rem(s + 1 + j, owners)
            send_or_keep(packed.at[o], coords1.at[mine], s_p, r_p, (o, y), o == s)

    pass_on(0)
    start_features(0)
    drain(coords1, r_p)
    end_features(coords1)
    drain(recv0, r_v.at[0])

    half = strata_here // 2

    def share(first_q, part):
        for q in range(2):
            row = coef1.at[y, first_q + q]
            above, below = lax.rem(y + 1, PLANES), lax.rem(y + PLANES - 1, PLANES)
            remote(row, row, s_c, r_c.at[part], (s, above)).start()
            remote(row, row, s_c, r_c.at[2 + part], (s, below)).start()

    for part in range(2):

        @pl.loop(0, half // 2)
        def _(g):
            for h in range(2):
                q = part * half + 2 * g + h
                rounded = refit(q, 0).astype(jnp.bfloat16)
                middle[q] = rounded
                coef1[y, q] = rounded

            @pl.when(g > 0)
            def _():
                share(part * half + 2 * g - 2, part)

        share(part * half + half - 2, part)

    pass_around(coef1, s, y, half, s_c, r_c)
    gathered(coef1, y, half, r_c)

    @pl.loop(0, members)
    def _(j):
        evaluate(turn(s, j, layers), 1, coef1)

        @pl.when(j > 0)
        def _():
            give_second(turn(s, j - 1, layers), 1)
            give_first(turn(s, j - 1, layers), 1)

    give_second(turn(s, members - 1, layers), 1)
    give_first(turn(s, members - 1, layers), 1)
    pass_on(1)
    start_features(1)
    drain(recv1, r_v.at[1])

    @pl.loop(0, strata_here)
    def _(q):
        first[q] = refit(q, 1)

    drain(coef1.at[pl.ds(0, PLANES - 1)], s_c)

    for step in range(STEPS):
        drain(packs.at[step, pl.ds(0, layers - 1)], s_z.at[step])

        @pl.when(own)
        def _():
            drain(recvs[step].at[pl.ds(0, owners - 1)], s_v.at[step])

        @pl.when(jnp.logical_not(own))
        def _():
            drain(recvs[step].at[pl.ds(0, owners)], s_v.at[step])

        @pl.when(relay)
        def _():
            drain(recvs[step].at[pl.ds(0, owners - layers // 2)], s_w.at[step])

        @pl.when(jnp.logical_not(relay))
        def _():
            drain(recvs[step].at[pl.ds(0, owners)], s_w.at[step])

    @pl.when(own)
    def _():
        drain(packed.at[pl.ds(0, owners - 1)], s_p)


VMEM = pl.BlockSpec(memory_space=pltpu.VMEM)
SMEM = pl.BlockSpec(memory_space=pltpu.SMEM)
DMA = pltpu.SemaphoreType.DMA
LIMIT = 60 * 1024 * 1024


def exchange(source, points, table, coef, rates, owners):
    members = owners // PLANES
    strata_here, local, _ = coef.shape
    return pl.pallas_call(
        exchange_kernel,
        out_shape=(
            jax.ShapeDtypeStruct((members, 24, BLOCK), jnp.bfloat16),
            jax.ShapeDtypeStruct((PLANES, strata_here, local, FEAT), jnp.bfloat16),
            jax.ShapeDtypeStruct((PLANES, local, BLOCK), jnp.float32),
            jax.ShapeDtypeStruct((owners // 8, 8, BLOCK), jnp.bfloat16),
            jax.ShapeDtypeStruct((PLANES, 8, BLOCK), jnp.float32),
        ),
        in_specs=[SMEM, VMEM, VMEM, VMEM, VMEM],
        out_specs=(VMEM,) * 5,
        scratch_shapes=[
            pltpu.VMEM((owners, 24, BLOCK), jnp.bfloat16),
            pltpu.VMEM((points.shape[2] // BLOCK, DIMS, BLOCK), jnp.bfloat16),
            pltpu.VMEM((8, BLOCK), jnp.float32),
        ]
        + [DMA] * 10
        + [DMA((6,))],
        compiler_params=pltpu.CompilerParams(
            collective_id=0, has_side_effects=True, vmem_limit_bytes=LIMIT
        ),
        name="exchange",
    )(source, points, table, coef, rates)


def main(room, codes, slots, source, lists, coords, coef_all, rates, start, points, owners):
    layers = owners // 8
    members = owners // PLANES
    _, strata_here, local, _ = coef_all.shape
    bf = jnp.bfloat16
    return pl.pallas_call(
        functools.partial(main_kernel, room),
        out_shape=(
            jax.ShapeDtypeStruct((strata_here, local, FEAT), bf),
            jax.ShapeDtypeStruct((strata_here, local, FEAT), jnp.float32),
        ),
        in_specs=[SMEM] * 4 + [VMEM] * 5,
        out_specs=(VMEM, VMEM),
        scratch_shapes=[
            pltpu.VMEM((members, FEAT, 2 * BLOCK), bf),
            pltpu.VMEM((strata_here * PATHS // (2 * BLOCK), FEAT, 2 * BLOCK), bf),
            pltpu.VMEM((STEPS, members, PLANES, local, BLOCK), bf),
            pltpu.VMEM((STEPS, members, PLANES, local, BLOCK), bf),
            pltpu.VMEM((layers, 8, local, BLOCK), bf),
            pltpu.VMEM((layers, 8, local, BLOCK), bf),
            pltpu.VMEM((STEPS, layers, room, local, BLOCK), bf),
            pltpu.VMEM((owners + layers * room, local, BLOCK), bf),
            pltpu.VMEM((owners + layers * room, local, BLOCK), bf),
            pltpu.VMEM((PLANES, strata_here, local, FEAT), bf),
            pltpu.VMEM((owners, 16, BLOCK), bf),
            pltpu.VMEM((points.shape[2] // BLOCK, DIMS, BLOCK), bf),
            pltpu.VMEM((members, 16, BLOCK), bf),
        ]
        + [DMA((STEPS,))] * 5
        + [DMA, DMA((6,)), DMA, DMA],
        compiler_params=pltpu.CompilerParams(
            collective_id=room, has_side_effects=True, vmem_limit_bytes=LIMIT
        ),
        name="steps",
    )(codes, slots, source, lists, coords, coef_all, rates, start, points)


def per_device(start_points, end_points, owner_lists, local_strata, last_coef, growth_rates):
    owners = lax.axis_size("strata")
    dev_blocks = owner_lists.shape[1]
    local = last_coef.shape[1]
    me = lax.axis_index("strata")
    block_iota = jnp.arange(dev_blocks, dtype=jnp.int32)
    slot_iota = jnp.arange(2 * owners, dtype=jnp.int32)
    rates = jnp.broadcast_to(growth_rates[:, None], (local, BLOCK))

    layers = owners // 8
    owner_ids = owner_lists[:, :, 0]
    earlier = (owner_ids[:, :, None] == owner_ids[:, None, :]) & (
        block_iota[None, None, :] < block_iota[None, :, None]
    )
    second = jnp.sum(earlier.astype(jnp.int32), axis=2)
    slots = owner_ids * 2 + second
    placing = slots[:, None, :] == slot_iota[None, :, None]
    source = jnp.sum(jnp.where(placing, block_iota[None, None, :], 0), axis=2)
    code = jnp.sum(jnp.where(placing, local_strata[:, None, :], 0), axis=2)
    ahead = (
        (second[:, None, :] == 1)
        & (owner_ids[:, :, None] // 8 == owner_ids[:, None, :] // 8)
        & (owner_ids[:, None, :] < owner_ids[:, :, None])
    )
    place = jnp.sum(ahead.astype(jnp.int32), axis=2)
    entry = jnp.where(second == 1, owner_ids // 8 * 8 + place, -1)
    listing = entry[:, None, :] == jnp.arange(owners, dtype=jnp.int32)[None, :, None]
    lists = jnp.sum(jnp.where(listing, owner_ids[:, None, :] % 8, 0), axis=2)
    over = jnp.max(jnp.where(second == 1, place, 0)) >= ROOM
    table = code.reshape(STEPS, owners, 2).transpose(0, 2, 1).reshape(2 * STEPS, owners)
    table = jnp.concatenate(
        [table, lists, jnp.broadcast_to(over.astype(jnp.int32), (2, owners))], axis=0
    )
    table = jnp.pad(table, ((0, 0), (0, BLOCK - owners))).astype(jnp.bfloat16)

    coords, coef_all, rates_all, tables, full = exchange(
        source[0], end_points, table, last_coef, rates, owners
    )
    here = jnp.arange(BLOCK, dtype=jnp.int32) == me
    arrived = coords[:, 16 : 16 + 2 * STEPS, :].astype(jnp.float32)
    codes = jnp.sum(jnp.where(here[None, None, :], arrived, 0.0), axis=2).astype(jnp.int32)
    codes = codes.reshape(-1, STEPS, 2).transpose(1, 0, 2).reshape(STEPS, -1)
    wanted = tables[:, 2 * STEPS : 3 * STEPS, :owners].astype(jnp.float32)
    wanted = wanted.reshape(layers, STEPS, layers, 8)
    at_layer = jnp.arange(layers, dtype=jnp.int32) == me // 8
    wanted = jnp.sum(jnp.where(at_layer[None, None, :, None], wanted, 0.0), axis=2)
    wanted = wanted.astype(jnp.int32).transpose(1, 0, 2).reshape(STEPS, layers * 8)
    crowded = jnp.max(full[:, 3 * STEPS, :]) > 0.5

    def run(room):
        index = jnp.where(second == 1, owners + owner_ids // 8 * room + place, owner_ids)
        return main(
            room,
            codes,
            index,
            source[1],
            wanted,
            coords,
            coef_all,
            rates_all.reshape(PLANES * local, BLOCK),
            start_points,
            end_points,
            owners,
        )

    return lax.cond(crowded, lambda: run(8), lambda: run(ROOM))


def solution(mesh):
    in_specs = (
        P(None, None, "strata"),
        P(None, None, "strata"),
        P(None, "strata", None),
        P(None, "strata"),
        P("strata", "comp", None),
        P("comp"),
    )
    out_specs = (P("strata", "comp", None), P("strata", "comp", None))
    return jax.shard_map(
        per_device, mesh=mesh, in_specs=in_specs, out_specs=out_specs, check_vma=False
    )
```
